32 devices in a mesh: grp: 2 (over y), seq: 4 (over z), head: 4 (over x, core).
Axes of the slice: x: 2, y: 2, z: 4, core: 2. Of those that a mesh axis runs over, the one named last changes fastest.
Arguments:
- queries: bfloat16 [8192, 2048], P(('grp', 'seq'), 'head'), parts along dimension 0, may hold values from -16.5 to 16.5
- keys: bfloat16 [8192, 2048], P(('grp', 'seq'), 'head'), parts along dimension 0, may hold values from -16.5 to 16.5
- values: bfloat16 [8192, 2048], P(('grp', 'seq'), 'head'), parts along dimension 0, may hold values from -6 to 6
- pattern: int32 [64, 15], P(('grp', 'seq')), parts along dimension 0, may hold values from 0 to 31, as said below
- out_weight: bfloat16 [2048, 2048], P('head'), may hold values from -0.5 to 0.5
Outputs:
- output: bfloat16 [8192, 2048], P(('grp', 'seq', 'head')), parts along dimension 0
The draws below stay inside these ranges and needn't reach their ends.
There are 2 independent parts, one for each index of `grp`. The reference program is written for one: setup_inputs(seed, part) draws one part's arguments, and reference() takes and returns one part's arrays. A program takes and returns all parts, laid end to end along the dimension named above; an argument that names none is the same for every part. Nothing has to cross between parts.
Inputs may be any that keep to these rules, and one draw needn't show every extreme that they name: `pattern`: row b lists first 7 distinct local blocks (b + o) mod 32 with -8 <= o <= 8, o = 0 always among them, then 8 distinct global blocks that are the same in every row.
All inputs are finite; a program needn't handle non-finite values.
Results may differ from the reference program's by a relative error of at most 0.0057.
Values may be sent and summed in bfloat16 or wider, within the bound.
No kernel may reach another device: no remote copies, remote signals or barrier semaphores. Data moves between devices by JAX's collectives and lax.ppermute only.
A program may use at most 128 MiB of HBM per device.

```python
import math
import jax
import jax.numpy as jnp
from jax import lax

D = 2048
HEADS = 16
DH = 128
BLK = 128
LOC = 7
GLB = 8
QB_DEV = 8
NSEL = 15
NBLK = 32
TOKENS = 4096


def pattern_parts(key):
    base = jax.random.fold_in(key, 7001)
    first_key, second_key = jax.random.split(base)
    span = 2 * QB_DEV
    ranks = jax.random.randint(first_key, (NBLK, span), 0, 1 << 20) * span + jnp.arange(span)
    order = jnp.argsort(ranks, axis=1, stable=True)[:, :LOC - 1]
    offsets = jnp.where(order < QB_DEV, order - QB_DEV, order - QB_DEV + 1)
    local = jnp.concatenate([jnp.zeros((NBLK, 1), jnp.int32), offsets.astype(jnp.int32)], axis=1)
    chosen = jax.random.permutation(second_key, NBLK)[:GLB].astype(jnp.int32)
    return (local, chosen)


def draw_pattern(key, part):
    local, chosen = pattern_parts(key)
    row_ids = jnp.arange(NBLK, dtype=jnp.int32)[:, None]
    local_ids = (row_ids + local) % NBLK
    global_ids = jnp.broadcast_to(chosen[None, :], (NBLK, GLB))
    return jnp.concatenate([local_ids, global_ids], axis=1).astype(jnp.int32)


def draw_keys(key, part):
    own_key = jax.random.fold_in(key, 7003)
    base = jnp.clip(jax.random.normal(own_key, (TOKENS, D), jnp.float32), -6.0, 6.0) * 1.4
    return base.astype(jnp.bfloat16)


def draw_queries(key, part):
    own_key = jax.random.fold_in(key, 7002)
    base = jnp.clip(jax.random.normal(own_key, (TOKENS, D), jnp.float32), -6.0, 6.0) * 1.4
    return base.astype(jnp.bfloat16)


def block_levels(key, dims, cuts, least, high):
    loudness = 1.0
    for position, shards_of in cuts:
        draws = jax.random.uniform(jax.random.fold_in(jax.random.fold_in(key, 6), position), (shards_of,), jnp.float32, least / len(cuts), high / len(cuts))
        loudness = loudness * jnp.repeat(jnp.exp(draws), dims[position] // shards_of).reshape((-1,) + (1,) * (len(dims) - 1 - position))
    return loudness


def bell_draw(stream_key, extent, deviation, reach, cuts=(), kind=jnp.bfloat16):
    values = jax.random.normal(stream_key, extent, jnp.float32) * deviation
    if len(cuts) > 0:
        values = block_levels(stream_key, extent, cuts, -0.22, 0.18) * values
    return jnp.clip(values, min=-reach, max=reach).astype(kind)


def setup_inputs(seed: int = 0, part: int = 0) -> dict:
    streams_of = jax.random.split(jax.random.key(seed), 6)
    part_keys = jax.random.split(jax.random.fold_in(streams_of[5], part), 6)
    return {
        "queries": draw_queries(jax.random.fold_in(jax.random.fold_in(streams_of[5], part), 71), part),
        "keys": draw_keys(jax.random.fold_in(jax.random.fold_in(streams_of[5], part), 71), part),
        "values": bell_draw(part_keys[2], (TOKENS, D), 1.0, 6.0, ((0, 4), (1, 4))),
        "pattern": draw_pattern(jax.random.fold_in(jax.random.fold_in(streams_of[5], part), 71), part),
        "out_weight": bell_draw(streams_of[4], (D, D), (D // 16) ** -0.5, 0.5, ((0, 4),)),
    }


def reference(queries, keys, values, pattern, out_weight):
    key_blocks = keys.reshape(NBLK, BLK, HEADS, DH)
    value_blocks = values.reshape(NBLK, BLK, HEADS, DH)
    query_blocks = queries.reshape(NBLK, BLK, HEADS, DH)
    scale = 1.0 / math.sqrt(DH)

    def one_block(inputs):
        query_blk, chosen = inputs
        key_set = jnp.take(key_blocks, chosen, axis=0).reshape(NSEL * BLK, HEADS, DH).astype(jnp.float32)
        value_set = jnp.take(value_blocks, chosen, axis=0).reshape(NSEL * BLK, HEADS, DH).astype(jnp.float32)
        scores = jnp.einsum('qhd,khd->hqk', query_blk.astype(jnp.float32), key_set) * scale
        peak = lax.optimization_barrier(jnp.max(scores, axis=-1, keepdims=True))
        expo = jnp.exp(scores - peak)
        denom = lax.optimization_barrier(jnp.sum(expo, axis=-1, keepdims=True))
        weights = lax.optimization_barrier((expo / denom).astype(jnp.bfloat16))
        mixed = jnp.einsum('hqk,khd->qhd', weights.astype(jnp.float32), value_set).astype(jnp.bfloat16)
        return jnp.dot(mixed.reshape(BLK, D), out_weight, preferred_element_type=jnp.float32).astype(jnp.bfloat16)
    result = lax.map(one_block, (query_blocks, pattern))
    return result.reshape(NBLK * BLK, D)
```

```python
import functools
import math

import jax
import jax.numpy as jnp
from jax import lax
from jax.experimental import pallas as pl
from jax.experimental.pallas import tpu as pltpu
from jax.sharding import PartitionSpec as P

DH = 128
BLK = 128
LOC = 7


def shifted(value, axis, steps):
    count = lax.axis_size(axis)
    return lax.ppermute(value, axis, [(i, (i + steps) % count) for i in range(count)])


def swapped(value, axis, mask):
    count = lax.axis_size(axis)
    return lax.ppermute(value, axis, [(i, i ^ mask) for i in range(count)])


def attend_body(count, slots, q_ref, *refs):
    pieces, (o_ref, kv, sems) = refs[:count], refs[count:]
    copies, first = [], 0
    for at, piece in enumerate(pieces):
        rows = pl.ds(first, piece.shape[1])
        copies.append(pltpu.make_async_copy(piece, kv.at[:, rows], sems.at[at]))
        first += piece.shape[1]
    for copy in copies:
        copy.start()
    for copy in copies:
        copy.wait()
    nsel = slots.shape[1]
    factor = math.log2(math.e) / math.sqrt(DH)

    def one_block(i, carry):
        rows = pl.ds(pl.multiple_of(i * BLK, BLK), BLK)
        picked = [
            pl.ds(pl.multiple_of(slots[i, j] * BLK, BLK), BLK) for j in range(nsel)
        ]
        key_set = jnp.concatenate([kv[0, p, :] for p in picked], axis=0)
        scores = lax.dot_general(
            q_ref[rows, :],
            key_set,
            (((1,), (1,)), ((), ())),
            preferred_element_type=jnp.float32,
        )
        peak = jnp.max(scores, axis=1, keepdims=True)
        expo = jnp.exp2(scores * factor - peak * factor).astype(jnp.bfloat16)
        ones = jnp.ones((BLK, DH), jnp.bfloat16)
        value_set = jnp.concatenate(
            [jnp.concatenate([kv[1, p, :], ones], axis=1) for p in picked], axis=0
        )
        mixed = jnp.dot(expo, value_set, preferred_element_type=jnp.float32)
        o_ref[rows, :] = (mixed[:, :DH] / mixed[:, DH:]).astype(o_ref.dtype)
        return carry

    lax.fori_loop(0, q_ref.shape[0] // BLK, one_block, 0)


def attend(queries, pieces, slots):
    total = sum(piece.shape[1] for piece in pieces)
    whole = pl.BlockSpec(queries.shape, lambda i, s: (0, 0))
    return pl.pallas_call(
        functools.partial(attend_body, len(pieces)),
        out_shape=jax.ShapeDtypeStruct(queries.shape, queries.dtype),
        grid_spec=pltpu.PrefetchScalarGridSpec(
            num_scalar_prefetch=1,
            grid=(1,),
            in_specs=[whole] + [pl.BlockSpec(memory_space=pl.ANY)] * len(pieces),
            out_specs=whole,
            scratch_shapes=[
                pltpu.VMEM((2, total, DH), queries.dtype),
                pltpu.SemaphoreType.DMA((len(pieces),)),
            ],
        ),
        compiler_params=pltpu.CompilerParams(vmem_limit_bytes=32 << 20),
        name="attend",
    )(slots, queries, *pieces)


def project_body(groups, count, has_part, final, at, *refs):
    lefts = refs[:groups]
    weights = refs[groups : groups + groups * count]
    rest = refs[groups + groups * count :]
    o_ref = rest[-1]
    total = rest[0][...] if has_part else None
    for g in range(groups):
        left = jnp.concatenate([lefts[g][j] for j in range(count)], axis=1)
        right = jnp.concatenate(
            [weights[g * count + j][...] for j in range(count)], axis=0
        )
        term = jnp.dot(left, right, preferred_element_type=jnp.float32)
        total = term if total is None else total + term
    o_ref[...] = total.astype(o_ref.dtype)


def project(lefts, weights, origins, part, dtype):
    groups, count = len(lefts), len(weights)
    _, rows, width = lefts[0].shape
    columns = weights[0].shape[1]
    tile = min(512, columns)

    def weight_spec(g):
        return pl.BlockSpec((width, tile), lambda n, at: (at[g], n))

    in_specs = [pl.BlockSpec((count, rows, width), lambda n, at: (0, 0, 0))] * groups
    operands = list(lefts)
    for g in range(groups):
        for weight in weights:
            in_specs.append(weight_spec(g))
            operands.append(weight)
    tile_spec = pl.BlockSpec((rows, tile), lambda n, at: (0, n))
    if part is not None:
        in_specs.append(tile_spec)
        operands.append(part)
    return pl.pallas_call(
        functools.partial(project_body, groups, count, part is not None, dtype),
        out_shape=jax.ShapeDtypeStruct((rows, columns), dtype),
        grid_spec=pltpu.PrefetchScalarGridSpec(
            num_scalar_prefetch=1,
            grid=(columns // tile,),
            in_specs=in_specs,
            out_specs=tile_spec,
        ),
        compiler_params=pltpu.CompilerParams(vmem_limit_bytes=32 << 20),
        name="project",
    )(jnp.stack(origins), *operands)


def by_heads(queries, keys, values, pattern, out_weight):
    qblocks = pattern.shape[0]
    rows, feat = queries.shape
    seq, heads = lax.axis_size("seq"), lax.axis_size("head")
    me, head = lax.axis_index("seq"), lax.axis_index("head")
    width = feat // seq
    share = rows // heads
    order = [1] + list(range(seq - 1, 1, -1))

    def columns_for(array, mask):
        return lax.dynamic_slice_in_dim(array, (me ^ mask) * width, width, axis=1)

    def pair_for(mask):
        return jnp.stack([columns_for(keys, mask), columns_for(values, mask)])

    pairs = {0: pair_for(0)}
    for mask in order:
        pairs[mask] = swapped(pair_for(mask), "seq", mask)
    patterns, asked = {0: pattern}, {0: columns_for(queries, 0)}
    for mask in order:
        patterns[mask] = swapped(pattern, "seq", mask)
    for mask in order:
        asked[mask] = swapped(columns_for(queries, mask), "seq", mask)
    weights = {0: out_weight}
    mask = 1
    while mask < heads:
        mask *= 2
    while mask > 1:
        mask //= 2
        for other in list(weights):
            weights[other ^ mask] = swapped(weights[other], "head", mask)

    pieces = [pairs[mask] for mask in range(seq)]
    ready = {}
    for mask in [0] + order:
        ids = patterns[mask]
        slots = ((ids // qblocks) ^ me) * qblocks + ids % qblocks
        mixed = attend(asked[mask], pieces, slots)
        mine = []
        for hop in range(heads):
            block = lax.dynamic_slice_in_dim(mixed, (head ^ hop) * share, share, axis=0)
            mine.append(swapped(block, "head", hop) if hop else block)
        stacked = jnp.stack(mine)
        ready[mask] = swapped(stacked, "seq", mask) if mask else stacked
    tail = order[-1]
    early = [mask for mask in [0] + order if mask != tail]
    ordered = [weights[hop] for hop in range(heads)]
    part = project(
        [ready[mask] for mask in early],
        ordered,
        [me ^ mask for mask in early],
        None,
        jnp.float32,
    )
    return project([ready[tail]], ordered, [me ^ tail], part, queries.dtype)


def by_rows(queries, keys, values, pattern, out_weight):
    qblocks = pattern.shape[0]
    rows, feat = queries.shape
    total = qblocks * lax.axis_size("seq")
    me = lax.axis_index("seq")
    own = jnp.stack([keys, values])
    nearby = [shifted(own, "seq", 1), own, shifted(own, "seq", -1)]
    ids = pattern[0, LOC:]
    local = ids - me * qblocks
    owned = (local >= 0) & (local < qblocks)
    blocks = own.reshape(2, qblocks, BLK, feat)
    picked = jnp.take(blocks, jnp.clip(local, 0, qblocks - 1), axis=1)
    picked = jnp.where(owned[None, :, None, None], picked, jnp.zeros((), picked.dtype))
    distant = lax.psum(picked, "seq").reshape(2, -1, feat)
    near_slots = (pattern[:, :LOC] - (me - 1) * qblocks) % total
    far_slots = jnp.broadcast_to(
        3 * qblocks + jnp.arange(ids.shape[0], dtype=jnp.int32), (qblocks, ids.shape[0])
    )
    slots = jnp.concatenate([near_slots, far_slots], axis=1)
    mixed = []
    for first in range(0, feat, DH):
        columns = slice(first, first + DH)
        pieces = [piece[:, :, columns] for piece in nearby + [distant]]
        mixed.append(attend(queries[:, columns], pieces, slots))
    attended = jnp.concatenate(mixed, axis=1)
    regrouped = lax.all_to_all(attended, "head", split_axis=0, concat_axis=1, tiled=True)
    result = jnp.dot(
        regrouped,
        lax.all_gather(out_weight, "head", axis=0, tiled=True),
        preferred_element_type=jnp.float32,
    )
    return result.astype(queries.dtype)


def per_device(queries, keys, values, pattern, out_weight):
    seq = lax.axis_size("seq")
    if queries.shape[1] == seq * DH and seq & (seq - 1) == 0:
        return by_heads(queries, keys, values, pattern, out_weight)
    return by_rows(queries, keys, values, pattern, out_weight)


def solution(mesh):
    placed = (
        P(("grp", "seq"), "head"),
        P(("grp", "seq"), "head"),
        P(("grp", "seq"), "head"),
        P(("grp", "seq"), None),
        P("head", None),
    )
    return jax.shard_map(
        per_device,
        mesh=mesh,
        in_specs=placed,
        out_specs=P(("grp", "seq", "head"), None),
        check_vma=False,
    )
```

```python
import functools
import math

import jax
import jax.numpy as jnp
from jax import lax
from jax.experimental import pallas as pl
from jax.experimental.pallas import tpu as pltpu
from jax.sharding import PartitionSpec as P


DH = 128
BLK = 128
LOC = 7


def shifted(value, axis, steps):
    count = lax.axis_size(axis)
    return lax.ppermute(value, axis, [(i, (i + steps) % count) for i in range(count)])


def swapped(value, axis, mask):
    count = lax.axis_size(axis)
    return lax.ppermute(value, axis, [(i, i ^ mask) for i in range(count)])


def chained(*values):
    return lax.optimization_barrier(values)


def attend_body(count, slots, q_ref, *refs):
    pieces, (o_ref, kv, sems) = refs[:count], refs[count:]
    copies, first = [], 0
    for at, piece in enumerate(pieces):
        rows = pl.ds(first, piece.shape[1])
        copies.append(pltpu.make_async_copy(piece, kv.at[:, rows], sems.at[at]))
        first += piece.shape[1]
    for copy in copies:
        copy.start()
    for copy in copies:
        copy.wait()
    nsel = slots.shape[1]
    factor = math.log2(math.e) / math.sqrt(DH)

    def one_block(i):
        rows = pl.ds(pl.multiple_of(i * BLK, BLK), BLK)
        picked = [
            pl.ds(pl.multiple_of(slots[i, j] * BLK, BLK), BLK) for j in range(nsel)
        ]
        key_set = jnp.concatenate([kv[0, p, :] for p in picked], axis=0)
        scores = lax.dot_general(
            q_ref[rows, :],
            key_set,
            (((1,), (1,)), ((), ())),
            preferred_element_type=jnp.float32,
        )
        peak = jnp.max(scores, axis=1, keepdims=True)
        expo = jnp.exp2(scores * factor - peak * factor).astype(jnp.bfloat16)
        ones = jnp.ones((BLK, DH), jnp.bfloat16)
        value_set = jnp.concatenate(
            [jnp.concatenate([kv[1, p, :], ones], axis=1) for p in picked], axis=0
        )
        mixed = jnp.dot(expo, value_set, preferred_element_type=jnp.float32)
        o_ref[rows, :] = (mixed[:, :DH] / mixed[:, DH:]).astype(o_ref.dtype)

    blocks = q_ref.shape[0] // BLK
    together = math.gcd(blocks, 8)

    def some_blocks(g, carry):
        for u in range(together):
            one_block(g * together + u)
        return carry

    lax.fori_loop(0, blocks // together, some_blocks, 0)


def attend(queries, pieces, slots):
    total = sum(piece.shape[1] for piece in pieces)
    whole = pl.BlockSpec(queries.shape, lambda i, s: (0, 0))
    return pl.pallas_call(
        functools.partial(attend_body, len(pieces)),
        out_shape=jax.ShapeDtypeStruct(queries.shape, queries.dtype),
        grid_spec=pltpu.PrefetchScalarGridSpec(
            num_scalar_prefetch=1,
            grid=(1,),
            in_specs=[whole] + [pl.BlockSpec(memory_space=pl.ANY)] * len(pieces),
            out_specs=whole,
            scratch_shapes=[
                pltpu.VMEM((2, total, DH), queries.dtype),
                pltpu.SemaphoreType.DMA((len(pieces),)),
            ],
        ),
        compiler_params=pltpu.CompilerParams(vmem_limit_bytes=32 << 20),
        name="attend",
    )(slots, queries, *pieces)


def project_body(groups, count, has_part, at, *refs):
    lefts = refs[:groups]
    weights = refs[groups : groups + groups * count]
    rest = refs[groups + groups * count :]
    o_ref = rest[-1]
    total = rest[0][...] if has_part else None
    for g in range(groups):
        left = jnp.concatenate([lefts[g][j] for j in range(count)], axis=1)
        right = jnp.concatenate(
            [weights[g * count + j][...] for j in range(count)], axis=0
        )
        term = jnp.dot(left, right, preferred_element_type=jnp.float32)
        total = term if total is None else total + term
    o_ref[...] = total.astype(o_ref.dtype)


def project(lefts, weights, origins, part, dtype):
    groups, count = len(lefts), len(weights)
    _, rows, width = lefts[0].shape
    columns = weights[0].shape[1]
    tile = min(512, columns)

    def weight_spec(g):
        return pl.BlockSpec((width, tile), lambda n, at: (at[g], n))

    in_specs = [pl.BlockSpec((count, rows, width), lambda n, at: (0, 0, 0))] * groups
    operands = list(lefts)
    for g in range(groups):
        for weight in weights:
            in_specs.append(weight_spec(g))
            operands.append(weight)
    tile_spec = pl.BlockSpec((rows, tile), lambda n, at: (0, n))
    if part is not None:
        in_specs.append(tile_spec)
        operands.append(part)
    return pl.pallas_call(
        functools.partial(project_body, groups, count, part is not None),
        out_shape=jax.ShapeDtypeStruct((rows, columns), dtype),
        grid_spec=pltpu.PrefetchScalarGridSpec(
            num_scalar_prefetch=1,
            grid=(columns // tile,),
            in_specs=in_specs,
            out_specs=tile_spec,
        ),
        compiler_params=pltpu.CompilerParams(vmem_limit_bytes=32 << 20),
        name="project",
    )(jnp.stack(origins), *operands)


def by_heads(queries, keys, values, pattern, out_weight):
    qblocks = pattern.shape[0]
    rows, feat = queries.shape
    seq, heads = lax.axis_size("seq"), lax.axis_size("head")
    me, head = lax.axis_index("seq"), lax.axis_index("head")
    width = feat // seq
    share = rows // heads
    order = plan_of(seq)

    def columns_for(array, mask):
        return lax.dynamic_slice_in_dim(array, (me ^ mask) * width, width, axis=1)

    def pair_for(mask):
        return jnp.stack([columns_for(keys, mask), columns_for(values, mask)])

    pairs = {0: pair_for(0)}
    patterns, asked = {0: pattern}, {0: columns_for(queries, 0)}
    for mask in order:
        pairs[mask] = swapped(pair_for(mask), "seq", mask)
        patterns[mask] = swapped(pattern, "seq", mask)
        asked[mask] = swapped(columns_for(queries, mask), "seq", mask)
    weights = {0: out_weight}
    for hop in far_first(heads):
        for other in list(weights):
            weights[other ^ hop] = swapped(weights[other], "head", hop)

    pieces = [pairs[mask] for mask in range(seq)]
    ready, before = {}, None
    for mask in order + [0]:
        ids = patterns[mask]
        slots = ((ids // qblocks) ^ me) * qblocks + ids % qblocks
        if before is not None:
            slots, before = chained(slots, before)
        mixed = before = attend(asked[mask], pieces, slots)
        mine = []
        for hop in range(heads):
            block = lax.dynamic_slice_in_dim(mixed, (head ^ hop) * share, share, axis=0)
            mine.append(swapped(block, "head", hop) if hop else block)
        stacked = jnp.stack(mine)
        ready[mask] = swapped(stacked, "seq", mask) if mask else stacked
    tail = order[-1]
    early = [mask for mask in [0] + order if mask != tail]
    ordered = [weights[hop] for hop in range(heads)]
    part = project(
        [ready[mask] for mask in early],
        ordered,
        [me ^ mask for mask in early],
        None,
        jnp.float32,
    )
    return project([ready[tail]], ordered, [me ^ tail], part, queries.dtype)


def plan_of(seq):
    return [seq - 1] + list(range(1, seq - 1))


def far_first(heads):
    hop = 1
    while hop < heads:
        hop *= 2
    hops = []
    while hop > 1:
        hop //= 2
        hops.append(hop)
    return hops


def by_rows(queries, keys, values, pattern, out_weight):
    qblocks = pattern.shape[0]
    _, feat = queries.shape
    total = qblocks * lax.axis_size("seq")
    me = lax.axis_index("seq")
    own = jnp.stack([keys, values])
    nearby = [shifted(own, "seq", 1), own, shifted(own, "seq", -1)]
    ids = pattern[0, LOC:]
    local = ids - me * qblocks
    owned = (local >= 0) & (local < qblocks)
    blocks = own.reshape(2, qblocks, BLK, feat)
    picked = jnp.take(blocks, jnp.clip(local, 0, qblocks - 1), axis=1)
    picked = jnp.where(owned[None, :, None, None], picked, jnp.zeros((), picked.dtype))
    distant = lax.psum(picked, "seq").reshape(2, -1, feat)
    near_slots = (pattern[:, :LOC] - (me - 1) * qblocks) % total
    far_slots = jnp.broadcast_to(
        3 * qblocks + jnp.arange(ids.shape[0], dtype=jnp.int32), (qblocks, ids.shape[0])
    )
    slots = jnp.concatenate([near_slots, far_slots], axis=1)
    mixed = []
    for first in range(0, feat, DH):
        columns = slice(first, first + DH)
        pieces = [piece[:, :, columns] for piece in nearby + [distant]]
        mixed.append(attend(queries[:, columns], pieces, slots))
    attended = jnp.concatenate(mixed, axis=1)
    regrouped = lax.all_to_all(attended, "head", split_axis=0, concat_axis=1, tiled=True)
    result = jnp.dot(
        regrouped,
        lax.all_gather(out_weight, "head", axis=0, tiled=True),
        preferred_element_type=jnp.float32,
    )
    return result.astype(queries.dtype)


def heads_split(feat, seq):
    return feat == seq * DH and seq & (seq - 1) == 0


def per_device(queries, keys, values, pattern, out_weight):
    if heads_split(queries.shape[1], lax.axis_size("seq")):
        return by_heads(queries, keys, values, pattern, out_weight)
    return by_rows(queries, keys, values, pattern, out_weight)


def solution(mesh):
    placed = (
        P(("grp", "seq"), "head"),
        P(("grp", "seq"), "head"),
        P(("grp", "seq"), "head"),
        P(("grp", "seq"), None),
        P("head", None),
    )
    step = jax.shard_map(
        per_device,
        mesh=mesh,
        in_specs=placed,
        out_specs=P(("grp", "seq", "head"), None),
        check_vma=False,
    )

    def run(queries, keys, values, pattern, out_weight):
        feat = queries.shape[1] // mesh.shape["head"]
        whole = step
        if heads_split(feat, mesh.shape["seq"]):
            whole = step
        return whole(queries, keys, values, pattern, out_weight)

    return run
```

```python
import functools
import math

import jax
import jax.numpy as jnp
from jax import lax
from jax.experimental import pallas as pl
from jax.experimental.pallas import tpu as pltpu
from jax.sharding import PartitionSpec as P


DH = 128
BLK = 128
LOC = 7


def shifted(value, axis, steps):
    count = lax.axis_size(axis)
    return lax.ppermute(value, axis, [(i, (i + steps) % count) for i in range(count)])


def swapped(value, axis, mask):
    count = lax.axis_size(axis)
    return lax.ppermute(value, axis, [(i, i ^ mask) for i in range(count)])


def swapped_by_parity(value, masks):
    seq, heads = lax.axis_size("seq"), lax.axis_size("head")
    moves = [
        (s * heads + h, (s ^ masks[h % 2]) * heads + h)
        for s in range(seq)
        for h in range(heads)
    ]
    return lax.ppermute(value, ("seq", "head"), moves)


def in_hbm(array):
    return pltpu.with_memory_space_constraint(array, pltpu.HBM)


def chained(*values):
    return lax.optimization_barrier(values)


def cut_body(plan, width, *refs):
    sources, rest = refs[:3], refs[3:]
    outs, sems = rest[:-1], rest[-1]
    me, even = lax.axis_index("seq"), lax.axis_index("head") % 2 == 0
    rows = sources[0].shape[0]
    part = math.gcd(rows, 256)
    copies = []
    for out, (which, masks) in zip(outs, plan):
        place = me ^ jnp.where(even, masks[0], masks[1])
        columns = pl.ds(pl.multiple_of(place * width, width), width)
        for at, source in enumerate(which):
            target = out if len(which) == 1 else out.at[at]
            for first in range(0, rows, part):
                strip = pl.ds(first, part)
                copies.append(
                    pltpu.make_async_copy(
                        sources[source].at[strip, columns],
                        target.at[strip],
                        sems.at[len(copies)],
                    )
                )
    for copy in copies:
        copy.start()
    for copy in copies:
        copy.wait()


def cut(arrays, plan, width):
    rows = arrays[0].shape[0]
    shapes = [
        (rows, width) if len(which) == 1 else (len(which), rows, width)
        for which, _ in plan
    ]
    strips = rows // math.gcd(rows, 256)
    count = sum(len(which) for which, _ in plan) * strips
    return pl.pallas_call(
        functools.partial(cut_body, plan, width),
        out_shape=[pltpu.VMEM(shape, arrays[0].dtype) for shape in shapes],
        in_specs=[pl.BlockSpec(memory_space=pl.ANY)] * len(arrays),
        out_specs=[pl.BlockSpec(memory_space=pltpu.VMEM)] * len(plan),
        scratch_shapes=[pltpu.SemaphoreType.DMA((count,))],
        compiler_params=pltpu.CompilerParams(vmem_limit_bytes=4 << 20),
        name="cut",
    )(*arrays)


def pool_body(count, *refs):
    pieces, kv, sems = refs[:count], refs[count], refs[count + 1]
    copies, first = [], 0
    for at, piece in enumerate(pieces):
        rows = pl.ds(first, piece.shape[1])
        copies.append(pltpu.make_async_copy(piece, kv.at[:, rows], sems.at[at]))
        first += piece.shape[1]
    for copy in copies:
        copy.start()
    for copy in copies:
        copy.wait()


def pool(pieces):
    total = sum(piece.shape[1] for piece in pieces)
    return pl.pallas_call(
        functools.partial(pool_body, len(pieces)),
        out_shape=pltpu.VMEM((2, total, DH), pieces[0].dtype),
        in_specs=[pl.BlockSpec(memory_space=pl.ANY)] * len(pieces),
        out_specs=pl.BlockSpec(memory_space=pltpu.VMEM),
        scratch_shapes=[pltpu.SemaphoreType.DMA((len(pieces),))],
        compiler_params=pltpu.CompilerParams(vmem_limit_bytes=4 << 20),
        name="pool",
    )(*[in_hbm(piece) for piece in pieces])


def attend_body(slots, q_ref, kv, o_ref):
    nsel = slots.shape[1]
    factor = math.log2(math.e) / math.sqrt(DH)

    def one_block(i):
        rows = pl.ds(pl.multiple_of(i * BLK, BLK), BLK)
        picked = [
            pl.ds(pl.multiple_of(slots[i, j] * BLK, BLK), BLK) for j in range(nsel)
        ]
        key_set = jnp.concatenate([kv[0, p, :] for p in picked], axis=0)
        scores = lax.dot_general(
            q_ref[rows, :],
            key_set,
            (((1,), (1,)), ((), ())),
            preferred_element_type=jnp.float32,
        )
        peak = jnp.max(scores, axis=1, keepdims=True)
        expo = jnp.exp2(scores * factor - peak * factor).astype(jnp.bfloat16)
        ones = jnp.ones((BLK, DH), jnp.bfloat16)
        value_set = jnp.concatenate(
            [jnp.concatenate([kv[1, p, :], ones], axis=1) for p in picked], axis=0
        )
        mixed = jnp.dot(expo, value_set, preferred_element_type=jnp.float32)
        o_ref[rows, :] = (mixed[:, :DH] / mixed[:, DH:]).astype(o_ref.dtype)

    blocks = q_ref.shape[0] // BLK
    together = math.gcd(blocks, 8)

    def some_blocks(g, carry):
        for u in range(together):
            one_block(g * together + u)
        return carry

    lax.fori_loop(0, blocks // together, some_blocks, 0)


def attend(queries, pooled, slots):
    return pl.pallas_call(
        attend_body,
        out_shape=jax.ShapeDtypeStruct(queries.shape, queries.dtype),
        in_specs=[
            pl.BlockSpec(memory_space=pltpu.SMEM),
            pl.BlockSpec(memory_space=pltpu.VMEM),
            pl.BlockSpec(memory_space=pltpu.VMEM),
        ],
        out_specs=pl.BlockSpec(memory_space=pltpu.VMEM),
        compiler_params=pltpu.CompilerParams(vmem_limit_bytes=24 << 20),
        name="attend",
    )(slots, queries, pooled)


def sheaf_body(count, width, *refs):
    sources, out, sems = refs[:count], refs[count], refs[count + 1]
    copies = []
    for origin in range(sources[0].shape[0] // width):
        for j, source in enumerate(sources):
            target = out.at[pl.ds((origin * count + j) * width, width)]
            copies.append(
                pltpu.make_async_copy(
                    source.at[pl.ds(origin * width, width)], target, sems.at[len(copies)]
                )
            )
    for copy in copies:
        copy.start()
    for copy in copies:
        copy.wait()


def sheaf(weights, width):
    count = len(weights)
    rows, columns = weights[0].shape
    return pl.pallas_call(
        functools.partial(sheaf_body, count, width),
        out_shape=pltpu.VMEM((count * rows, columns), weights[0].dtype),
        in_specs=[pl.BlockSpec(memory_space=pl.ANY)] * count,
        out_specs=pl.BlockSpec(memory_space=pltpu.VMEM),
        scratch_shapes=[pltpu.SemaphoreType.DMA((count * (rows // width),))],
        compiler_params=pltpu.CompilerParams(vmem_limit_bytes=4 << 20),
        name="sheaf",
    )(*[in_hbm(weight) for weight in weights])


def product(left_ref, rights_ref, mask, columns):
    count, _, width = left_ref.shape
    origin = lax.axis_index("seq") ^ mask
    depth = count * width
    left = jnp.concatenate([left_ref[j] for j in range(count)], axis=1)
    right = rights_ref[pl.ds(pl.multiple_of(origin * depth, depth), depth), columns]
    return jnp.dot(left, right, preferred_element_type=jnp.float32)


def project_body(masks, tile, rights_ref, *refs):
    lefts, o_ref = refs[:-1], refs[-1]
    for first in range(0, o_ref.shape[1], tile):
        columns = pl.ds(first, tile)
        total = None
        for left_ref, mask in zip(lefts, masks):
            term = product(left_ref, rights_ref, mask, columns)
            total = term if total is None else total + term
        o_ref[:, columns] = total


def project(lefts, masks, rights):
    rows, columns = lefts[0].shape[1], rights.shape[1]
    inside = pl.BlockSpec(memory_space=pltpu.VMEM)
    return pl.pallas_call(
        functools.partial(project_body, masks, math.gcd(512, columns)),
        out_shape=pltpu.VMEM((rows, columns), jnp.float32),
        in_specs=[inside] * (1 + len(lefts)),
        out_specs=inside,
        compiler_params=pltpu.CompilerParams(vmem_limit_bytes=24 << 20),
        name="project",
    )(rights, *lefts)


def finish_body(mask, tile, left_ref, rights_ref, part_ref, o_ref, held, sems):
    copies = []
    for n in range(part_ref.shape[1] // tile):
        columns = pl.ds(n * tile, tile)
        term = product(left_ref, rights_ref, mask, columns)
        held[:, columns] = (part_ref[:, columns] + term).astype(held.dtype)
        copies.append(
            pltpu.make_async_copy(held.at[:, columns], o_ref.at[:, columns], sems.at[n])
        )
        copies[-1].start()
    for copy in copies:
        copy.wait()


def finish(left, mask, rights, part, dtype):
    tile = math.gcd(512, part.shape[1])
    inside = pl.BlockSpec(memory_space=pltpu.VMEM)
    return pl.pallas_call(
        functools.partial(finish_body, mask, tile),
        out_shape=jax.ShapeDtypeStruct(part.shape, dtype),
        in_specs=[inside] * 3,
        out_specs=pl.BlockSpec(memory_space=pl.ANY),
        scratch_shapes=[
            pltpu.VMEM(part.shape, dtype),
            pltpu.SemaphoreType.DMA((part.shape[1] // tile,)),
        ],
        compiler_params=pltpu.CompilerParams(vmem_limit_bytes=24 << 20),
        name="finish",
    )(left, rights, part)


def rounds_of(seq):
    even = list(range(1, seq))
    odd = even[:2][::-1] + even[2:]
    return list(zip(even, odd))


def served_by(seq):
    far = list(range(seq - 1, 1, -1))
    return far[:1] + [1] + far[1:]


def far_first(heads):
    hops = [1]
    while 2 * hops[0] < heads:
        hops = [2 * hops[0]] + hops
    return hops


def by_heads(queries, keys, values, pattern, out_weight):
    qblocks = pattern.shape[0]
    rows, feat = queries.shape
    seq, heads = lax.axis_size("seq"), lax.axis_size("head")
    me, head = lax.axis_index("seq"), lax.axis_index("head")
    width = feat // seq
    share = rows // heads
    rounds, order = rounds_of(seq), served_by(seq)
    even = head % 2 == 0
    arrays = tuple(in_hbm(array) for array in (keys, values, queries))

    pairs = []
    for masks in rounds:
        (outgoing,) = cut(arrays, [((0, 1), masks)], width)
        pairs.append(swapped_by_parity(outgoing, masks))
    kept = [((0, 1), (0, 0)), ((2,), (0, 0))] + [((2,), (m, m)) for m in order]
    own_pair, own_queries, *queries_for = cut(arrays, kept, width)
    pairs = [own_pair] + pairs
    patterns, asked = {0: pattern}, {0: own_queries}
    for at, mask in enumerate(order):
        patterns[mask] = swapped(pattern, "seq", mask)
        asked[mask] = swapped(queries_for[at], "seq", mask)
    weights = {0: out_weight}
    for hop in far_first(heads):
        for other in list(weights):
            weights[other ^ hop] = swapped(weights[other], "head", hop)

    pooled = pool(pairs)

    def slots_of(ids):
        apart = (ids // qblocks) ^ me
        slot = jnp.zeros_like(ids)
        for r, (a, b) in enumerate(rounds):
            slot = jnp.where(apart == jnp.where(even, a, b), r + 1, slot)
        return slot * qblocks + ids % qblocks

    def split(block):
        got = []
        for hop in range(heads):
            mine = lax.dynamic_slice_in_dim(block, (head ^ hop) * share, share, axis=0)
            got.append(swapped(mine, "head", hop) if hop else mine)
        return jnp.stack(got)

    ready, before = {}, None
    for mask in [0] + order:
        slots = slots_of(patterns[mask])
        if before is not None:
            slots, before = chained(slots, before)
        mixed = before = attend(asked[mask], pooled, slots)
        if mask and mask != 1 and mask != order[-1]:
            ready[mask] = split(swapped(mixed, "seq", mask))
        elif mask:
            ready[mask] = swapped(split(mixed), "seq", mask)
        else:
            ready[mask] = split(mixed)
    tail = order[-1]
    early = [mask for mask in [0] + order if mask != tail]
    rights = sheaf([weights[hop] for hop in range(heads)], width)
    part = project([ready[mask] for mask in early], early, rights)
    return finish(ready[tail], tail, rights, part, queries.dtype)


def by_rows(queries, keys, values, pattern, out_weight):
    qblocks = pattern.shape[0]
    _, feat = queries.shape
    total = qblocks * lax.axis_size("seq")
    me = lax.axis_index("seq")
    own = jnp.stack([keys, values])
    nearby = [shifted(own, "seq", 1), own, shifted(own, "seq", -1)]
    ids = pattern[0, LOC:]
    local = ids - me * qblocks
    owned = (local >= 0) & (local < qblocks)
    blocks = own.reshape(2, qblocks, BLK, feat)
    picked = jnp.take(blocks, jnp.clip(local, 0, qblocks - 1), axis=1)
    picked = jnp.where(owned[None, :, None, None], picked, jnp.zeros((), picked.dtype))
    distant = lax.psum(picked, "seq").reshape(2, -1, feat)
    near_slots = (pattern[:, :LOC] - (me - 1) * qblocks) % total
    far_slots = jnp.broadcast_to(
        3 * qblocks + jnp.arange(ids.shape[0], dtype=jnp.int32), (qblocks, ids.shape[0])
    )
    slots = jnp.concatenate([near_slots, far_slots], axis=1)
    mixed = []
    for first in range(0, feat, DH):
        columns = slice(first, first + DH)
        pooled = pool([piece[:, :, columns] for piece in nearby + [distant]])
        mixed.append(attend(queries[:, columns], pooled, slots))
    attended = jnp.concatenate(mixed, axis=1)
    regrouped = lax.all_to_all(attended, "head", split_axis=0, concat_axis=1, tiled=True)
    result = jnp.dot(
        regrouped,
        lax.all_gather(out_weight, "head", axis=0, tiled=True),
        preferred_element_type=jnp.float32,
    )
    return result.astype(queries.dtype)


def heads_split(feat, seq):
    return feat == seq * DH and seq & (seq - 1) == 0


def per_device(queries, keys, values, pattern, out_weight):
    if heads_split(queries.shape[1], lax.axis_size("seq")):
        return by_heads(queries, keys, values, pattern, out_weight)
    return by_rows(queries, keys, values, pattern, out_weight)


def solution(mesh):
    placed = (
        P(("grp", "seq"), "head"),
        P(("grp", "seq"), "head"),
        P(("grp", "seq"), "head"),
        P(("grp", "seq"), None),
        P("head", None),
    )
    step = jax.shard_map(
        per_device,
        mesh=mesh,
        in_specs=placed,
        out_specs=P(("grp", "seq", "head"), None),
        check_vma=False,
    )

    def run(queries, keys, values, pattern, out_weight):
        feat = queries.shape[1] // mesh.shape["head"]
        whole = step
        if heads_split(feat, mesh.shape["seq"]):
            whole = step
        return whole(queries, keys, values, pattern, out_weight)

    return run
```

```python
import functools
import math

import jax
import jax.numpy as jnp
from jax import lax
from jax.experimental import pallas as pl
from jax.experimental.pallas import tpu as pltpu
from jax.sharding import PartitionSpec as P


DH = 128
BLK = 128
LOC = 7


def shifted(value, axis, steps):
    count = lax.axis_size(axis)
    return lax.ppermute(value, axis, [(i, (i + steps) % count) for i in range(count)])


def swapped(value, axis, mask):
    count = lax.axis_size(axis)
    return lax.ppermute(value, axis, [(i, i ^ mask) for i in range(count)])


def sent(value, masks, hop):
    seq, heads = lax.axis_size("seq"), lax.axis_size("head")
    moves = [
        (s * heads + h, (s ^ masks[h % 2]) * heads + (h ^ hop))
        for s in range(seq)
        for h in range(heads)
    ]
    return lax.ppermute(value, ("seq", "head"), moves)


def in_hbm(array):
    return pltpu.with_memory_space_constraint(array, pltpu.HBM)


def chained(*values):
    return lax.optimization_barrier(values)


def cut_body(plan, width, *refs):
    sources, rest = refs[:3], refs[3:]
    outs, sems = rest[:-1], rest[-1]
    me, even = lax.axis_index("seq"), lax.axis_index("head") % 2 == 0
    rows = sources[0].shape[0]
    part = math.gcd(rows, 256)
    copies = []
    for out, (which, masks) in zip(outs, plan):
        place = me ^ jnp.where(even, masks[0], masks[1])
        columns = pl.ds(pl.multiple_of(place * width, width), width)
        for at, source in enumerate(which):
            target = out if len(which) == 1 else out.at[at]
            for first in range(0, rows, part):
                strip = pl.ds(first, part)
                copies.append(
                    pltpu.make_async_copy(
                        sources[source].at[strip, columns],
                        target.at[strip],
                        sems.at[len(copies)],
                    )
                )
    for copy in copies:
        copy.start()
    for copy in copies:
        copy.wait()


def cut(arrays, plan, width):
    rows = arrays[0].shape[0]
    shapes = [
        (rows, width) if len(which) == 1 else (len(which), rows, width)
        for which, _ in plan
    ]
    strips = rows // math.gcd(rows, 256)
    count = sum(len(which) for which, _ in plan) * strips
    return pl.pallas_call(
        functools.partial(cut_body, plan, width),
        out_shape=[pltpu.VMEM(shape, arrays[0].dtype) for shape in shapes],
        in_specs=[pl.BlockSpec(memory_space=pl.ANY)] * len(arrays),
        out_specs=[pl.BlockSpec(memory_space=pltpu.VMEM)] * len(plan),
        scratch_shapes=[pltpu.SemaphoreType.DMA((count,))],
        compiler_params=pltpu.CompilerParams(vmem_limit_bytes=4 << 20),
        name="cut",
    )(*arrays)


def pool_body(count, *refs):
    pieces, kv, sems = refs[:count], refs[count], refs[count + 1]
    copies, first = [], 0
    for at, piece in enumerate(pieces):
        rows = pl.ds(first, piece.shape[1])
        copies.append(pltpu.make_async_copy(piece, kv.at[:, rows], sems.at[at]))
        first += piece.shape[1]
    for copy in copies:
        copy.start()
    for copy in copies:
        copy.wait()


def pool(pieces):
    total = sum(piece.shape[1] for piece in pieces)
    return pl.pallas_call(
        functools.partial(pool_body, len(pieces)),
        out_shape=pltpu.VMEM((2, total, DH), pieces[0].dtype),
        in_specs=[pl.BlockSpec(memory_space=pl.ANY)] * len(pieces),
        out_specs=pl.BlockSpec(memory_space=pltpu.VMEM),
        scratch_shapes=[pltpu.SemaphoreType.DMA((len(pieces),))],
        compiler_params=pltpu.CompilerParams(vmem_limit_bytes=4 << 20),
        name="pool",
    )(*[in_hbm(piece) for piece in pieces])


def attend_body(slots, q_ref, kv, o_ref):
    nsel = slots.shape[1]
    factor = math.log2(math.e) / math.sqrt(DH)

    def one_block(i):
        rows = pl.ds(pl.multiple_of(i * BLK, BLK), BLK)
        picked = [
            pl.ds(pl.multiple_of(slots[i, j] * BLK, BLK), BLK) for j in range(nsel)
        ]
        key_set = jnp.concatenate([kv[0, p, :] for p in picked], axis=0)
        scores = lax.dot_general(
            q_ref[rows, :],
            key_set,
            (((1,), (1,)), ((), ())),
            preferred_element_type=jnp.float32,
        )
        peak = jnp.max(scores, axis=1, keepdims=True)
        expo = jnp.exp2(scores * factor - peak * factor).astype(jnp.bfloat16)
        ones = jnp.ones((BLK, DH), jnp.bfloat16)
        value_set = jnp.concatenate(
            [jnp.concatenate([kv[1, p, :], ones], axis=1) for p in picked], axis=0
        )
        mixed = jnp.dot(expo, value_set, preferred_element_type=jnp.float32)
        o_ref[rows, :] = (mixed[:, :DH] / mixed[:, DH:]).astype(o_ref.dtype)

    blocks = q_ref.shape[0] // BLK
    together = math.gcd(blocks, 8)

    def some_blocks(g, carry):
        for u in range(together):
            one_block(g * together + u)
        return carry

    lax.fori_loop(0, blocks // together, some_blocks, 0)


def attend(queries, pooled, slots):
    return pl.pallas_call(
        attend_body,
        out_shape=jax.ShapeDtypeStruct(queries.shape, queries.dtype),
        in_specs=[
            pl.BlockSpec(memory_space=pltpu.SMEM),
            pl.BlockSpec(memory_space=pltpu.VMEM),
            pl.BlockSpec(memory_space=pltpu.VMEM),
        ],
        out_specs=pl.BlockSpec(memory_space=pltpu.VMEM),
        compiler_params=pltpu.CompilerParams(vmem_limit_bytes=24 << 20),
        name="attend",
    )(slots, queries, pooled)


def sheaf_body(count, width, *refs):
    sources, out, sems = refs[:count], refs[count], refs[count + 1]
    copies = []
    for origin in range(sources[0].shape[0] // width):
        for j, source in enumerate(sources):
            target = out.at[pl.ds((origin * count + j) * width, width)]
            copies.append(
                pltpu.make_async_copy(
                    source.at[pl.ds(origin * width, width)], target, sems.at[len(copies)]
                )
            )
    for copy in copies:
        copy.start()
    for copy in copies:
        copy.wait()


def sheaf(weights, width):
    count = len(weights)
    rows, columns = weights[0].shape
    return pl.pallas_call(
        functools.partial(sheaf_body, count, width),
        out_shape=pltpu.VMEM((count * rows, columns), weights[0].dtype),
        in_specs=[pl.BlockSpec(memory_space=pl.ANY)] * count,
        out_specs=pl.BlockSpec(memory_space=pltpu.VMEM),
        scratch_shapes=[pltpu.SemaphoreType.DMA((count * (rows // width),))],
        compiler_params=pltpu.CompilerParams(vmem_limit_bytes=4 << 20),
        name="sheaf",
    )(*weights)


def product(left_refs, rights_ref, mask, columns):
    origin = lax.axis_index("seq") ^ mask
    depth = len(left_refs) * left_refs[0].shape[1]
    left = jnp.concatenate([ref[...] for ref in left_refs], axis=1)
    right = rights_ref[pl.ds(pl.multiple_of(origin * depth, depth), depth), columns]
    return jnp.dot(left, right, preferred_element_type=jnp.float32)


def project_body(masks, count, tile, rights_ref, *refs):
    lefts, o_ref = refs[:-1], refs[-1]
    for first in range(0, o_ref.shape[1], tile):
        columns = pl.ds(first, tile)
        total = None
        for at, mask in enumerate(masks):
            group = lefts[at * count : (at + 1) * count]
            term = product(group, rights_ref, mask, columns)
            total = term if total is None else total + term
        o_ref[:, columns] = total


def project(lefts, masks, rights):
    count = len(lefts[0])
    rows, columns = lefts[0][0].shape[0], rights.shape[1]
    inside = pl.BlockSpec(memory_space=pltpu.VMEM)
    return pl.pallas_call(
        functools.partial(project_body, masks, count, math.gcd(512, columns)),
        out_shape=pltpu.VMEM((rows, columns), jnp.float32),
        in_specs=[inside] * (1 + len(lefts) * count),
        out_specs=inside,
        compiler_params=pltpu.CompilerParams(vmem_limit_bytes=24 << 20),
        name="project",
    )(rights, *[block for group in lefts for block in group])


def finish_body(mask, tile, rights_ref, part_ref, *refs):
    lefts, (o_ref, held, sems) = refs[:-3], refs[-3:]
    copies = []
    for n in range(part_ref.shape[1] // tile):
        columns = pl.ds(n * tile, tile)
        term = product(lefts, rights_ref, mask, columns)
        held[:, columns] = (part_ref[:, columns] + term).astype(held.dtype)
        copies.append(
            pltpu.make_async_copy(held.at[:, columns], o_ref.at[:, columns], sems.at[n])
        )
        copies[-1].start()
    for copy in copies:
        copy.wait()


def finish(lefts, mask, rights, part, dtype):
    tile = math.gcd(512, part.shape[1])
    inside = pl.BlockSpec(memory_space=pltpu.VMEM)
    return pl.pallas_call(
        functools.partial(finish_body, mask, tile),
        out_shape=jax.ShapeDtypeStruct(part.shape, dtype),
        in_specs=[inside] * (2 + len(lefts)),
        out_specs=pl.BlockSpec(memory_space=pl.ANY),
        scratch_shapes=[
            pltpu.VMEM(part.shape, dtype),
            pltpu.SemaphoreType.DMA((part.shape[1] // tile,)),
        ],
        compiler_params=pltpu.CompilerParams(vmem_limit_bytes=24 << 20),
        name="finish",
    )(rights, part, *lefts)


def rounds_of(seq):
    even = list(range(1, seq))
    odd = even[:2][::-1] + even[2:]
    return list(zip(even, odd))


def served_by(seq):
    far = list(range(seq - 1, 1, -1))
    return far[:1] + [1] + far[1:]


def far_first(heads):
    hops = [1]
    while 2 * hops[0] < heads:
        hops = [2 * hops[0]] + hops
    return hops


def by_heads(queries, keys, values, pattern, out_weight):
    qblocks = pattern.shape[0]
    rows, feat = queries.shape
    seq, heads = lax.axis_size("seq"), lax.axis_size("head")
    me, head = lax.axis_index("seq"), lax.axis_index("head")
    width = feat // seq
    share = rows // heads
    rounds, order = rounds_of(seq), served_by(seq)
    even = head % 2 == 0
    arrays = tuple(in_hbm(array) for array in (keys, values, queries))

    pairs = []
    for masks in rounds:
        (outgoing,) = cut(arrays, [((0, 1), masks)], width)
        pairs.append(sent(outgoing, masks, 0))
    kept = [((0, 1), (0, 0)), ((2,), (0, 0))] + [((2,), (m, m)) for m in order]
    own_pair, own_queries, *queries_for = cut(arrays, kept, width)
    pairs = [own_pair] + pairs
    patterns, asked = {0: pattern}, {0: own_queries}
    for at, mask in enumerate(order):
        patterns[mask] = swapped(pattern, "seq", mask)
        asked[mask] = swapped(queries_for[at], "seq", mask)
    weights = {0: out_weight}
    for hop in far_first(heads):
        for other in list(weights):
            weights[other ^ hop] = swapped(weights[other], "head", hop)

    pooled = pool(pairs)

    def slots_of(ids):
        apart = (ids // qblocks) ^ me
        slot = jnp.zeros_like(ids)
        for r, (a, b) in enumerate(rounds):
            slot = jnp.where(apart == jnp.where(even, a, b), r + 1, slot)
        return slot * qblocks + ids % qblocks

    def split(block, mask):
        got = []
        for hop in range(heads):
            mine = lax.dynamic_slice_in_dim(block, (head ^ hop) * share, share, axis=0)
            if mask or hop:
                mine = sent(mine, (mask, mask), hop)
            got.append(mine)
        return got

    ready, before = {}, None
    for mask in [0] + order:
        slots = slots_of(patterns[mask])
        if before is not None:
            slots, before = chained(slots, before)
        mixed = before = attend(asked[mask], pooled, slots)
        ready[mask] = split(mixed, mask)
    tail = order[-1]
    early = [mask for mask in [0] + order if mask != tail]
    rights = sheaf([weights[hop] for hop in range(heads)], width)
    part = project([ready[mask] for mask in early], early, rights)
    return finish(ready[tail], tail, rights, part, queries.dtype)


def by_rows(queries, keys, values, pattern, out_weight):
    qblocks = pattern.shape[0]
    _, feat = queries.shape
    total = qblocks * lax.axis_size("seq")
    me = lax.axis_index("seq")
    own = jnp.stack([keys, values])
    nearby = [shifted(own, "seq", 1), own, shifted(own, "seq", -1)]
    ids = pattern[0, LOC:]
    local = ids - me * qblocks
    owned = (local >= 0) & (local < qblocks)
    blocks = own.reshape(2, qblocks, BLK, feat)
    picked = jnp.take(blocks, jnp.clip(local, 0, qblocks - 1), axis=1)
    picked = jnp.where(owned[None, :, None, None], picked, jnp.zeros((), picked.dtype))
    distant = lax.psum(picked, "seq").reshape(2, -1, feat)
    near_slots = (pattern[:, :LOC] - (me - 1) * qblocks) % total
    far_slots = jnp.broadcast_to(
        3 * qblocks + jnp.arange(ids.shape[0], dtype=jnp.int32), (qblocks, ids.shape[0])
    )
    slots = jnp.concatenate([near_slots, far_slots], axis=1)
    mixed = []
    for first in range(0, feat, DH):
        columns = slice(first, first + DH)
        pooled = pool([piece[:, :, columns] for piece in nearby + [distant]])
        mixed.append(attend(queries[:, columns], pooled, slots))
    attended = jnp.concatenate(mixed, axis=1)
    regrouped = lax.all_to_all(attended, "head", split_axis=0, concat_axis=1, tiled=True)
    result = jnp.dot(
        regrouped,
        lax.all_gather(out_weight, "head", axis=0, tiled=True),
        preferred_element_type=jnp.float32,
    )
    return result.astype(queries.dtype)


def heads_split(feat, seq):
    return feat == seq * DH and seq & (seq - 1) == 0


def per_device(queries, keys, values, pattern, out_weight):
    if heads_split(queries.shape[1], lax.axis_size("seq")):
        return by_heads(queries, keys, values, pattern, out_weight)
    return by_rows(queries, keys, values, pattern, out_weight)


def solution(mesh):
    placed = (
        P(("grp", "seq"), "head"),
        P(("grp", "seq"), "head"),
        P(("grp", "seq"), "head"),
        P(("grp", "seq"), None),
        P("head", None),
    )
    step = jax.shard_map(
        per_device,
        mesh=mesh,
        in_specs=placed,
        out_specs=P(("grp", "seq", "head"), None),
        check_vma=False,
    )

    def run(queries, keys, values, pattern, out_weight):
        feat = queries.shape[1] // mesh.shape["head"]
        whole = step
        if heads_split(feat, mesh.shape["seq"]):
            whole = step
        return whole(queries, keys, values, pattern, out_weight)

    return run
```

```python
import functools
import math

import jax
import jax.numpy as jnp
from jax import lax
from jax.experimental import pallas as pl
from jax.experimental.pallas import tpu as pltpu
from jax.sharding import PartitionSpec as P


DH = 128
BLK = 128
LOC = 7


def shifted(value, axis, steps):
    count = lax.axis_size(axis)
    return lax.ppermute(value, axis, [(i, (i + steps) % count) for i in range(count)])


def swapped(value, axis, mask):
    count = lax.axis_size(axis)
    return lax.ppermute(value, axis, [(i, i ^ mask) for i in range(count)])


def sent(value, masks, hop):
    seq, heads = lax.axis_size("seq"), lax.axis_size("head")
    moves = [
        (s * heads + h, (s ^ masks[h % 2]) * heads + (h ^ hop))
        for s in range(seq)
        for h in range(heads)
    ]
    return lax.ppermute(value, ("seq", "head"), moves)


def in_hbm(array):
    return pltpu.with_memory_space_constraint(array, pltpu.HBM)


def chained(*values):
    return lax.optimization_barrier(values)


def cut_body(plan, width, *refs):
    sources, rest = refs[:3], refs[3:]
    outs, sems = rest[:-1], rest[-1]
    me, even = lax.axis_index("seq"), lax.axis_index("head") % 2 == 0
    rows = sources[0].shape[0]
    part = math.gcd(rows, 256)
    copies = []
    for out, (which, masks) in zip(outs, plan):
        place = me ^ jnp.where(even, masks[0], masks[1])
        columns = pl.ds(pl.multiple_of(place * width, width), width)
        for at, source in enumerate(which):
            target = out if len(which) == 1 else out.at[at]
            for first in range(0, rows, part):
                strip = pl.ds(first, part)
                copies.append(
                    pltpu.make_async_copy(
                        sources[source].at[strip, columns],
                        target.at[strip],
                        sems.at[len(copies)],
                    )
                )
    for copy in copies:
        copy.start()
    for copy in copies:
        copy.wait()


def cut(arrays, plan, width):
    rows = arrays[0].shape[0]
    shapes = [
        (rows, width) if len(which) == 1 else (len(which), rows, width)
        for which, _ in plan
    ]
    strips = rows // math.gcd(rows, 256)
    count = sum(len(which) for which, _ in plan) * strips
    return pl.pallas_call(
        functools.partial(cut_body, plan, width),
        out_shape=[pltpu.VMEM(shape, arrays[0].dtype) for shape in shapes],
        in_specs=[pl.BlockSpec(memory_space=pl.ANY)] * len(arrays),
        out_specs=[pl.BlockSpec(memory_space=pltpu.VMEM)] * len(plan),
        scratch_shapes=[pltpu.SemaphoreType.DMA((count,))],
        compiler_params=pltpu.CompilerParams(vmem_limit_bytes=4 << 20),
        name="cut",
    )(*arrays)


def pool_body(count, *refs):
    pieces, kv, sems = refs[:count], refs[count], refs[count + 1]
    copies, first = [], 0
    for at, piece in enumerate(pieces):
        rows = pl.ds(first, piece.shape[1])
        copies.append(pltpu.make_async_copy(piece, kv.at[:, rows], sems.at[at]))
        first += piece.shape[1]
    for copy in copies:
        copy.start()
    for copy in copies:
        copy.wait()


def pool(pieces):
    total = sum(piece.shape[1] for piece in pieces)
    return pl.pallas_call(
        functools.partial(pool_body, len(pieces)),
        out_shape=pltpu.VMEM((2, total, DH), pieces[0].dtype),
        in_specs=[pl.BlockSpec(memory_space=pl.ANY)] * len(pieces),
        out_specs=pl.BlockSpec(memory_space=pltpu.VMEM),
        scratch_shapes=[pltpu.SemaphoreType.DMA((len(pieces),))],
        compiler_params=pltpu.CompilerParams(vmem_limit_bytes=4 << 20),
        name="pool",
    )(*[in_hbm(piece) for piece in pieces])


def attend_body(slots, q_ref, kv, o_ref):
    nsel = slots.shape[1]
    factor = math.log2(math.e) / math.sqrt(DH)

    def one_block(i):
        rows = pl.ds(pl.multiple_of(i * BLK, BLK), BLK)
        picked = [
            pl.ds(pl.multiple_of(slots[i, j] * BLK, BLK), BLK) for j in range(nsel)
        ]
        key_set = jnp.concatenate([kv[0, p, :] for p in picked], axis=0)
        scores = lax.dot_general(
            q_ref[rows, :],
            key_set,
            (((1,), (1,)), ((), ())),
            preferred_element_type=jnp.float32,
        )
        peak = jnp.max(scores, axis=1, keepdims=True)
        expo = jnp.exp2(scores * factor - peak * factor).astype(jnp.bfloat16)
        ones = jnp.ones((BLK, DH), jnp.bfloat16)
        value_set = jnp.concatenate(
            [jnp.concatenate([kv[1, p, :], ones], axis=1) for p in picked], axis=0
        )
        mixed = jnp.dot(expo, value_set, preferred_element_type=jnp.float32)
        o_ref[rows, :] = (mixed[:, :DH] / mixed[:, DH:]).astype(o_ref.dtype)

    blocks = q_ref.shape[0] // BLK
    together = math.gcd(blocks, 8)

    def some_blocks(g, carry):
        for u in range(together):
            one_block(g * together + u)
        return carry

    lax.fori_loop(0, blocks // together, some_blocks, 0)


def attend(queries, pooled, slots):
    return pl.pallas_call(
        attend_body,
        out_shape=jax.ShapeDtypeStruct(queries.shape, queries.dtype),
        in_specs=[
            pl.BlockSpec(memory_space=pltpu.SMEM),
            pl.BlockSpec(memory_space=pltpu.VMEM),
            pl.BlockSpec(memory_space=pltpu.VMEM),
        ],
        out_specs=pl.BlockSpec(memory_space=pltpu.VMEM),
        compiler_params=pltpu.CompilerParams(vmem_limit_bytes=24 << 20),
        name="attend",
    )(slots, queries, pooled)


def sheaf_body(count, width, *refs):
    sources, out, sems = refs[:count], refs[count], refs[count + 1]
    copies = []
    for origin in range(sources[0].shape[0] // width):
        for j, source in enumerate(sources):
            target = out.at[pl.ds((origin * count + j) * width, width)]
            copies.append(
                pltpu.make_async_copy(
                    source.at[pl.ds(origin * width, width)], target, sems.at[len(copies)]
                )
            )
    for copy in copies:
        copy.start()
    for copy in copies:
        copy.wait()


def sheaf(weights, width):
    count = len(weights)
    rows, columns = weights[0].shape
    return pl.pallas_call(
        functools.partial(sheaf_body, count, width),
        out_shape=pltpu.VMEM((count * rows, columns), weights[0].dtype),
        in_specs=[pl.BlockSpec(memory_space=pl.ANY)] * count,
        out_specs=pl.BlockSpec(memory_space=pltpu.VMEM),
        scratch_shapes=[pltpu.SemaphoreType.DMA((count * (rows // width),))],
        compiler_params=pltpu.CompilerParams(vmem_limit_bytes=4 << 20),
        name="sheaf",
    )(*weights)


def product(left_refs, rights_ref, masks, columns):
    me, head = lax.axis_index("seq"), lax.axis_index("head")
    count, width = len(left_refs), left_refs[0].shape[1]
    rights = []
    for hop in range(count):
        origin = me ^ jnp.where((head + hop) % 2 == 0, masks[0], masks[1])
        first = pl.multiple_of((origin * count + hop) * width, width)
        rights.append(rights_ref[pl.ds(first, width), columns])
    left = jnp.concatenate([ref[...] for ref in left_refs], axis=1)
    right = jnp.concatenate(rights, axis=0)
    return jnp.dot(left, right, preferred_element_type=jnp.float32)


def project_body(masks, count, tile, rights_ref, *refs):
    lefts, o_ref = refs[:-1], refs[-1]
    for first in range(0, o_ref.shape[1], tile):
        columns = pl.ds(first, tile)
        total = None
        for at, mask in enumerate(masks):
            group = lefts[at * count : (at + 1) * count]
            term = product(group, rights_ref, mask, columns)
            total = term if total is None else total + term
        o_ref[:, columns] = total


def project(lefts, masks, rights):
    count = len(lefts[0])
    rows, columns = lefts[0][0].shape[0], rights.shape[1]
    inside = pl.BlockSpec(memory_space=pltpu.VMEM)
    return pl.pallas_call(
        functools.partial(project_body, masks, count, math.gcd(512, columns)),
        out_shape=pltpu.VMEM((rows, columns), jnp.float32),
        in_specs=[inside] * (1 + len(lefts) * count),
        out_specs=inside,
        compiler_params=pltpu.CompilerParams(vmem_limit_bytes=24 << 20),
        name="project",
    )(rights, *[block for group in lefts for block in group])


def finish_body(mask, tile, rights_ref, part_ref, *refs):
    lefts, (o_ref, held, sems) = refs[:-3], refs[-3:]
    copies = []
    for n in range(part_ref.shape[1] // tile):
        columns = pl.ds(n * tile, tile)
        term = product(lefts, rights_ref, mask, columns)
        held[:, columns] = (part_ref[:, columns] + term).astype(held.dtype)
        copies.append(
            pltpu.make_async_copy(held.at[:, columns], o_ref.at[:, columns], sems.at[n])
        )
        copies[-1].start()
    for copy in copies:
        copy.wait()


def finish(lefts, mask, rights, part, dtype):
    tile = math.gcd(512, part.shape[1])
    inside = pl.BlockSpec(memory_space=pltpu.VMEM)
    return pl.pallas_call(
        functools.partial(finish_body, mask, tile),
        out_shape=jax.ShapeDtypeStruct(part.shape, dtype),
        in_specs=[inside] * (2 + len(lefts)),
        out_specs=pl.BlockSpec(memory_space=pl.ANY),
        scratch_shapes=[
            pltpu.VMEM(part.shape, dtype),
            pltpu.SemaphoreType.DMA((part.shape[1] // tile,)),
        ],
        compiler_params=pltpu.CompilerParams(vmem_limit_bytes=24 << 20),
        name="finish",
    )(rights, part, *lefts)


def rounds_of(seq):
    even = list(range(1, seq))
    odd = even[:2][::-1] + even[2:]
    return list(zip(even, odd))


def served_by(seq):
    far = list(range(seq - 1, 1, -1))
    even = far[:1] + [1] + far[1:]
    odd = even[:1] + even[1:3][::-1] + even[3:]
    return [(0, 0)] + list(zip(even, odd))


def far_first(heads):
    hops = [1]
    while 2 * hops[0] < heads:
        hops = [2 * hops[0]] + hops
    return hops


def by_heads(queries, keys, values, pattern, out_weight):
    qblocks = pattern.shape[0]
    rows, feat = queries.shape
    seq, heads = lax.axis_size("seq"), lax.axis_size("head")
    me, head = lax.axis_index("seq"), lax.axis_index("head")
    width = feat // seq
    share = rows // heads
    rounds, order = rounds_of(seq), served_by(seq)
    even = head % 2 == 0
    arrays = tuple(in_hbm(array) for array in (keys, values, queries))

    pairs = []
    for masks in rounds:
        (outgoing,) = cut(arrays, [((0, 1), masks)], width)
        pairs.append(sent(outgoing, masks, 0))
    kept = [((0, 1), (0, 0))] + [((2,), masks) for masks in order]
    own_pair, *queries_for = cut(arrays, kept, width)
    pairs = [own_pair] + pairs
    patterns, asked = [pattern], [queries_for[0]]
    for at, masks in enumerate(order[1:], 1):
        patterns.append(sent(pattern, masks, 0))
        asked.append(sent(queries_for[at], masks, 0))
    weights = {0: out_weight}
    for hop in far_first(heads):
        for other in list(weights):
            weights[other ^ hop] = swapped(weights[other], "head", hop)

    pooled = pool(pairs)

    def slots_of(ids):
        apart = (ids // qblocks) ^ me
        slot = jnp.zeros_like(ids)
        for r, (a, b) in enumerate(rounds):
            slot = jnp.where(apart == jnp.where(even, a, b), r + 1, slot)
        return slot * qblocks + ids % qblocks

    def split(block, at):
        got = []
        for hop in range(heads):
            mine = lax.dynamic_slice_in_dim(block, (head ^ hop) * share, share, axis=0)
            if at or hop:
                mine = sent(mine, order[at], hop)
            got.append(mine)
        return got

    ready, before = [], None
    for at in range(len(order)):
        slots = slots_of(patterns[at])
        if before is not None:
            slots, before = chained(slots, before)
        mixed = before = attend(asked[at], pooled, slots)
        ready.append(split(mixed, at))
    rights = sheaf([weights[hop] for hop in range(heads)], width)
    part = project(ready[:-1], order[:-1], rights)
    return finish(ready[-1], order[-1], rights, part, queries.dtype)


def by_rows(queries, keys, values, pattern, out_weight):
    qblocks = pattern.shape[0]
    _, feat = queries.shape
    total = qblocks * lax.axis_size("seq")
    me = lax.axis_index("seq")
    own = jnp.stack([keys, values])
    nearby = [shifted(own, "seq", 1), own, shifted(own, "seq", -1)]
    ids = pattern[0, LOC:]
    local = ids - me * qblocks
    owned = (local >= 0) & (local < qblocks)
    blocks = own.reshape(2, qblocks, BLK, feat)
    picked = jnp.take(blocks, jnp.clip(local, 0, qblocks - 1), axis=1)
    picked = jnp.where(owned[None, :, None, None], picked, jnp.zeros((), picked.dtype))
    distant = lax.psum(picked, "seq").reshape(2, -1, feat)
    near_slots = (pattern[:, :LOC] - (me - 1) * qblocks) % total
    far_slots = jnp.broadcast_to(
        3 * qblocks + jnp.arange(ids.shape[0], dtype=jnp.int32), (qblocks, ids.shape[0])
    )
    slots = jnp.concatenate([near_slots, far_slots], axis=1)
    mixed = []
    for first in range(0, feat, DH):
        columns = slice(first, first + DH)
        pooled = pool([piece[:, :, columns] for piece in nearby + [distant]])
        mixed.append(attend(queries[:, columns], pooled, slots))
    attended = jnp.concatenate(mixed, axis=1)
    regrouped = lax.all_to_all(attended, "head", split_axis=0, concat_axis=1, tiled=True)
    result = jnp.dot(
        regrouped,
        lax.all_gather(out_weight, "head", axis=0, tiled=True),
        preferred_element_type=jnp.float32,
    )
    return result.astype(queries.dtype)


def heads_split(feat, seq):
    return feat == seq * DH and seq & (seq - 1) == 0


def per_device(queries, keys, values, pattern, out_weight):
    if heads_split(queries.shape[1], lax.axis_size("seq")):
        return by_heads(queries, keys, values, pattern, out_weight)
    return by_rows(queries, keys, values, pattern, out_weight)


def solution(mesh):
    placed = (
        P(("grp", "seq"), "head"),
        P(("grp", "seq"), "head"),
        P(("grp", "seq"), "head"),
        P(("grp", "seq"), None),
        P("head", None),
    )
    step = jax.shard_map(
        per_device,
        mesh=mesh,
        in_specs=placed,
        out_specs=P(("grp", "seq", "head"), None),
        check_vma=False,
    )

    def run(queries, keys, values, pattern, out_weight):
        feat = queries.shape[1] // mesh.shape["head"]
        whole = step
        if heads_split(feat, mesh.shape["seq"]):
            whole = step
        return whole(queries, keys, values, pattern, out_weight)

    return run
```

```python
import functools
import math

import jax
import jax.numpy as jnp
from jax import lax
from jax.experimental import pallas as pl
from jax.experimental.pallas import tpu as pltpu
from jax.sharding import PartitionSpec as P


DH = 128
BLK = 128
LOC = 7


def shifted(value, axis, steps):
    count = lax.axis_size(axis)
    return lax.ppermute(value, axis, [(i, (i + steps) % count) for i in range(count)])


def swapped(value, axis, mask):
    count = lax.axis_size(axis)
    return lax.ppermute(value, axis, [(i, i ^ mask) for i in range(count)])


def sent(value, masks, hop):
    seq, heads = lax.axis_size("seq"), lax.axis_size("head")
    moves = [
        (s * heads + h, (s ^ masks[h % 2]) * heads + (h ^ hop))
        for s in range(seq)
        for h in range(heads)
    ]
    return lax.ppermute(value, ("seq", "head"), moves)


def in_hbm(array):
    return pltpu.with_memory_space_constraint(array, pltpu.HBM)


def chained(*values):
    return lax.optimization_barrier(values)


def cut_body(plan, width, *refs):
    sources, rest = refs[:3], refs[3:]
    outs, sems = rest[:-1], rest[-1]
    me, even = lax.axis_index("seq"), lax.axis_index("head") % 2 == 0
    rows = sources[0].shape[0]
    part = math.gcd(rows, 256)
    copies = []
    for out, (which, masks) in zip(outs, plan):
        place = me ^ jnp.where(even, masks[0], masks[1])
        columns = pl.ds(pl.multiple_of(place * width, width), width)
        for at, source in enumerate(which):
            target = out if len(which) == 1 else out.at[at]
            for first in range(0, rows, part):
                strip = pl.ds(first, part)
                copies.append(
                    pltpu.make_async_copy(
                        sources[source].at[strip, columns],
                        target.at[strip],
                        sems.at[len(copies)],
                    )
                )
    for copy in copies:
        copy.start()
    for copy in copies:
        copy.wait()


def cut(arrays, plan, width):
    rows = arrays[0].shape[0]
    shapes = [
        (rows, width) if len(which) == 1 else (len(which), rows, width)
        for which, _ in plan
    ]
    strips = rows // math.gcd(rows, 256)
    count = sum(len(which) for which, _ in plan) * strips
    return pl.pallas_call(
        functools.partial(cut_body, plan, width),
        out_shape=[pltpu.VMEM(shape, arrays[0].dtype) for shape in shapes],
        in_specs=[pl.BlockSpec(memory_space=pl.ANY)] * len(arrays),
        out_specs=[pl.BlockSpec(memory_space=pltpu.VMEM)] * len(plan),
        scratch_shapes=[pltpu.SemaphoreType.DMA((count,))],
        compiler_params=pltpu.CompilerParams(vmem_limit_bytes=4 << 20),
        name="cut",
    )(*arrays)


def pool_body(count, *refs):
    pieces, kv, sems = refs[:count], refs[count], refs[count + 1]
    copies, first = [], 0
    for at, piece in enumerate(pieces):
        rows = pl.ds(first, piece.shape[1])
        copies.append(pltpu.make_async_copy(piece, kv.at[:, rows], sems.at[at]))
        first += piece.shape[1]
    for copy in copies:
        copy.start()
    for copy in copies:
        copy.wait()


def pool(pieces):
    total = sum(piece.shape[1] for piece in pieces)
    return pl.pallas_call(
        functools.partial(pool_body, len(pieces)),
        out_shape=pltpu.VMEM((2, total, DH), pieces[0].dtype),
        in_specs=[pl.BlockSpec(memory_space=pl.ANY)] * len(pieces),
        out_specs=pl.BlockSpec(memory_space=pltpu.VMEM),
        scratch_shapes=[pltpu.SemaphoreType.DMA((len(pieces),))],
        compiler_params=pltpu.CompilerParams(vmem_limit_bytes=4 << 20),
        name="pool",
    )(*[in_hbm(piece) for piece in pieces])


def attend_body(slots, q_ref, kv, o_ref):
    nsel = slots.shape[1]
    factor = math.log2(math.e) / math.sqrt(DH)

    def one_block(i):
        rows = pl.ds(pl.multiple_of(i * BLK, BLK), BLK)
        picked = [
            pl.ds(pl.multiple_of(slots[i, j] * BLK, BLK), BLK) for j in range(nsel)
        ]
        key_set = jnp.concatenate([kv[0, p, :] for p in picked], axis=0)
        scores = lax.dot_general(
            q_ref[rows, :],
            key_set,
            (((1,), (1,)), ((), ())),
            preferred_element_type=jnp.float32,
        )
        peak = jnp.max(scores, axis=1, keepdims=True)
        expo = jnp.exp2(scores * factor - peak * factor).astype(jnp.bfloat16)
        ones = jnp.ones((BLK, DH), jnp.bfloat16)
        value_set = jnp.concatenate(
            [jnp.concatenate([kv[1, p, :], ones], axis=1) for p in picked], axis=0
        )
        mixed = jnp.dot(expo, value_set, preferred_element_type=jnp.float32)
        o_ref[rows, :] = (mixed[:, :DH] / mixed[:, DH:]).astype(o_ref.dtype)

    blocks = q_ref.shape[0] // BLK
    together = math.gcd(blocks, 8)

    def some_blocks(g, carry):
        for u in range(together):
            one_block(g * together + u)
        return carry

    lax.fori_loop(0, blocks // together, some_blocks, 0)


def attend(queries, pooled, slots):
    return pl.pallas_call(
        attend_body,
        out_shape=jax.ShapeDtypeStruct(queries.shape, queries.dtype),
        in_specs=[
            pl.BlockSpec(memory_space=pltpu.SMEM),
            pl.BlockSpec(memory_space=pltpu.VMEM),
            pl.BlockSpec(memory_space=pltpu.VMEM),
        ],
        out_specs=pl.BlockSpec(memory_space=pltpu.VMEM),
        compiler_params=pltpu.CompilerParams(vmem_limit_bytes=24 << 20),
        name="attend",
    )(slots, queries, pooled)


def sheaf_body(count, width, *refs):
    sources, out, sems = refs[:count], refs[count], refs[count + 1]
    copies = []
    for origin in range(sources[0].shape[0] // width):
        for j, source in enumerate(sources):
            target = out.at[pl.ds((origin * count + j) * width, width)]
            copies.append(
                pltpu.make_async_copy(
                    source.at[pl.ds(origin * width, width)], target, sems.at[len(copies)]
                )
            )
    for copy in copies:
        copy.start()
    for copy in copies:
        copy.wait()


def sheaf(weights, width):
    count = len(weights)
    rows, columns = weights[0].shape
    return pl.pallas_call(
        functools.partial(sheaf_body, count, width),
        out_shape=pltpu.VMEM((count * rows, columns), weights[0].dtype),
        in_specs=[pl.BlockSpec(memory_space=pl.ANY)] * count,
        out_specs=pl.BlockSpec(memory_space=pltpu.VMEM),
        scratch_shapes=[pltpu.SemaphoreType.DMA((count * (rows // width),))],
        compiler_params=pltpu.CompilerParams(vmem_limit_bytes=4 << 20),
        name="sheaf",
    )(*weights)


def product(left_refs, rights_ref, masks, columns):
    me, head = lax.axis_index("seq"), lax.axis_index("head")
    count, width = len(left_refs), left_refs[0].shape[1]
    rights = []
    for hop in range(count):
        origin = me ^ jnp.where((head + hop) % 2 == 0, masks[0], masks[1])
        first = pl.multiple_of((origin * count + hop) * width, width)
        rights.append(rights_ref[pl.ds(first, width), columns])
    left = jnp.concatenate([ref[...] for ref in left_refs], axis=1)
    right = jnp.concatenate(rights, axis=0)
    return jnp.dot(left, right, preferred_element_type=jnp.float32)


def project_body(masks, count, tile, rights_ref, *refs):
    lefts, o_ref = refs[:-1], refs[-1]
    for first in range(0, o_ref.shape[1], tile):
        columns = pl.ds(first, tile)
        total = None
        for at, mask in enumerate(masks):
            group = lefts[at * count : (at + 1) * count]
            term = product(group, rights_ref, mask, columns)
            total = term if total is None else total + term
        o_ref[:, columns] = total


def project(lefts, masks, rights):
    count = len(lefts[0])
    rows, columns = lefts[0][0].shape[0], rights.shape[1]
    inside = pl.BlockSpec(memory_space=pltpu.VMEM)
    return pl.pallas_call(
        functools.partial(project_body, masks, count, math.gcd(512, columns)),
        out_shape=pltpu.VMEM((rows, columns), jnp.float32),
        in_specs=[inside] * (1 + len(lefts) * count),
        out_specs=inside,
        compiler_params=pltpu.CompilerParams(vmem_limit_bytes=24 << 20),
        name="project",
    )(rights, *[block for group in lefts for block in group])


def finish_body(mask, tile, rights_ref, part_ref, *refs):
    lefts, (o_ref, held, sems) = refs[:-3], refs[-3:]
    copies = []
    for n in range(part_ref.shape[1] // tile):
        columns = pl.ds(n * tile, tile)
        term = product(lefts, rights_ref, mask, columns)
        held[:, columns] = (part_ref[:, columns] + term).astype(held.dtype)
        copies.append(
            pltpu.make_async_copy(held.at[:, columns], o_ref.at[:, columns], sems.at[n])
        )
        copies[-1].start()
    for copy in copies:
        copy.wait()


def finish(lefts, mask, rights, part, dtype):
    tile = math.gcd(512, part.shape[1])
    inside = pl.BlockSpec(memory_space=pltpu.VMEM)
    return pl.pallas_call(
        functools.partial(finish_body, mask, tile),
        out_shape=jax.ShapeDtypeStruct(part.shape, dtype),
        in_specs=[inside] * (2 + len(lefts)),
        out_specs=pl.BlockSpec(memory_space=pl.ANY),
        scratch_shapes=[
            pltpu.VMEM(part.shape, dtype),
            pltpu.SemaphoreType.DMA((part.shape[1] // tile,)),
        ],
        compiler_params=pltpu.CompilerParams(vmem_limit_bytes=24 << 20),
        name="finish",
    )(rights, part, *lefts)


def rounds_of(seq):
    even = list(range(1, seq))
    odd = even[:2][::-1] + even[2:]
    return list(zip(even, odd))


def served_by(seq):
    far = list(range(seq - 1, 1, -1))
    even = far[:1] + [1] + far[1:]
    odd = even[2:3] + even[:2] + even[3:]
    return [(0, 0)] + list(zip(even, odd))


def far_first(heads):
    hops = [1]
    while 2 * hops[0] < heads:
        hops = [2 * hops[0]] + hops
    return hops


def by_heads(queries, keys, values, pattern, out_weight):
    qblocks = pattern.shape[0]
    rows, feat = queries.shape
    seq, heads = lax.axis_size("seq"), lax.axis_size("head")
    me, head = lax.axis_index("seq"), lax.axis_index("head")
    width = feat // seq
    share = rows // heads
    rounds, order = rounds_of(seq), served_by(seq)
    even = head % 2 == 0
    arrays = tuple(in_hbm(array) for array in (keys, values, queries))

    first = cut(arrays, [((0, 1), rounds[0])], width)
    more = cut(arrays, [((0, 1), masks) for masks in rounds[1:]], width)
    pairs = [
        sent(outgoing, masks, 0)
        for outgoing, masks in zip([*first, *more], rounds)
    ]
    kept = [((0, 1), (0, 0))] + [((2,), masks) for masks in order]
    own_pair, *queries_for = cut(arrays, kept, width)
    pairs = [own_pair] + pairs
    patterns, asked = [pattern], [queries_for[0]]
    for at, masks in enumerate(order[1:], 1):
        patterns.append(sent(pattern, masks, 0))
        asked.append(sent(queries_for[at], masks, 0))
    weights = {0: out_weight}
    for hop in far_first(heads):
        for other in list(weights):
            weights[other ^ hop] = swapped(weights[other], "head", hop)

    pooled = pool(pairs)

    def slots_of(ids):
        apart = (ids // qblocks) ^ me
        slot = jnp.zeros_like(ids)
        for r, (a, b) in enumerate(rounds):
            slot = jnp.where(apart == jnp.where(even, a, b), r + 1, slot)
        return slot * qblocks + ids % qblocks

    def split(block, at):
        got = []
        for hop in range(heads):
            mine = lax.dynamic_slice_in_dim(block, (head ^ hop) * share, share, axis=0)
            if at or hop:
                mine = sent(mine, order[at], hop)
            got.append(mine)
        return got

    ready, before = [], None
    for at in range(len(order)):
        slots = slots_of(patterns[at])
        if before is not None:
            slots, before = chained(slots, before)
        mixed = before = attend(asked[at], pooled, slots)
        ready.append(split(mixed, at))
    rights = sheaf([weights[hop] for hop in range(heads)], width)
    part = project(ready[:-1], order[:-1], rights)
    return finish(ready[-1], order[-1], rights, part, queries.dtype)


def by_rows(queries, keys, values, pattern, out_weight):
    qblocks = pattern.shape[0]
    _, feat = queries.shape
    total = qblocks * lax.axis_size("seq")
    me = lax.axis_index("seq")
    own = jnp.stack([keys, values])
    nearby = [shifted(own, "seq", 1), own, shifted(own, "seq", -1)]
    ids = pattern[0, LOC:]
    local = ids - me * qblocks
    owned = (local >= 0) & (local < qblocks)
    blocks = own.reshape(2, qblocks, BLK, feat)
    picked = jnp.take(blocks, jnp.clip(local, 0, qblocks - 1), axis=1)
    picked = jnp.where(owned[None, :, None, None], picked, jnp.zeros((), picked.dtype))
    distant = lax.psum(picked, "seq").reshape(2, -1, feat)
    near_slots = (pattern[:, :LOC] - (me - 1) * qblocks) % total
    far_slots = jnp.broadcast_to(
        3 * qblocks + jnp.arange(ids.shape[0], dtype=jnp.int32), (qblocks, ids.shape[0])
    )
    slots = jnp.concatenate([near_slots, far_slots], axis=1)
    mixed = []
    for first in range(0, feat, DH):
        columns = slice(first, first + DH)
        pooled = pool([piece[:, :, columns] for piece in nearby + [distant]])
        mixed.append(attend(queries[:, columns], pooled, slots))
    attended = jnp.concatenate(mixed, axis=1)
    regrouped = lax.all_to_all(attended, "head", split_axis=0, concat_axis=1, tiled=True)
    result = jnp.dot(
        regrouped,
        lax.all_gather(out_weight, "head", axis=0, tiled=True),
        preferred_element_type=jnp.float32,
    )
    return result.astype(queries.dtype)


def heads_split(feat, seq):
    return feat == seq * DH and seq & (seq - 1) == 0


def per_device(queries, keys, values, pattern, out_weight):
    if heads_split(queries.shape[1], lax.axis_size("seq")):
        return by_heads(queries, keys, values, pattern, out_weight)
    return by_rows(queries, keys, values, pattern, out_weight)


def solution(mesh):
    placed = (
        P(("grp", "seq"), "head"),
        P(("grp", "seq"), "head"),
        P(("grp", "seq"), "head"),
        P(("grp", "seq"), None),
        P("head", None),
    )
    step = jax.shard_map(
        per_device,
        mesh=mesh,
        in_specs=placed,
        out_specs=P(("grp", "seq", "head"), None),
        check_vma=False,
    )

    def run(queries, keys, values, pattern, out_weight):
        feat = queries.shape[1] // mesh.shape["head"]
        whole = step
        if heads_split(feat, mesh.shape["seq"]):
            whole = step
        return whole(queries, keys, values, pattern, out_weight)

    return run
```
